512 devices in a mesh: pool: 32 (over z_hi, y), ctx: 4 (over x), head: 4 (over z_lo, core).
Axes of the slice: x: 4, y: 8, z: 8 (z_hi: 4, z_lo: 2; z = z_hi * 2 + z_lo), core: 2. Of those that a mesh axis runs over, the one named last changes fastest.
Arguments:
- kv_pool: bfloat16 [4, 1024, 2, 32, 1024], P('ctx', 'pool', None, None, 'head'), may hold values from -6 to 6
- state_pool: bfloat16 [1024, 64, 1024], P('pool', 'ctx', 'head'), may hold values from -0.59765625 to 0.59765625
- block_owner: int32 [4, 1024], P('ctx'), may hold values from 0 to 31, as said below
- block_index: int32 [4, 1024], P('ctx'), may hold values from 0 to 31, as said below
- history_len: int32 [32], P('pool'), may hold values from 1 to 4096, as said below
- turn_len: int32 [32], P('pool'), may hold values from 256 to 512, as said below
- mixer_in: bfloat16 [32, 128, 64, 512], P('pool', 'head', 'ctx'), may hold values from -6 to 6
- input_proj: bfloat16 [32, 8, 256, 512], P('pool', 'head'), may hold values from -1.5 to 1.5
- output_proj: bfloat16 [32, 8, 256, 512], P('pool', 'head'), may hold values from -6 to 6
- step_size: float32 [32, 128, 512], P('pool', 'head'), may hold values from 0 to 2, as said below
- decay_rate: float32 [128], P('head'), may hold values from 0 to 4, as said below
- bypass_factor: float32 [128], P('head'), may hold values from 0.5 to 1.5
- queries: bfloat16 [32, 512, 8192], P('pool', 'ctx', 'head'), may hold values from -300 to 300
- turn_kv: bfloat16 [32, 2, 512, 1024], P('pool', None, 'ctx', 'head'), may hold values from -6 to 6
Outputs:
- mixer_out: bfloat16 [32, 128, 64, 512], P('pool', 'head', 'ctx')
- next_state: float32 [32, 128, 64, 256], P('pool', 'head', 'ctx')
- attn_out: bfloat16 [32, 512, 8192], P('pool', 'ctx', 'head')
The draws below stay inside these ranges and needn't reach their ends.
Inputs may be any that keep to these rules, and one draw needn't show every extreme that they name: `block_owner`: in each row c, every session owns exactly 32 slots, and each aligned run of 32 slots (one pool shard) holds at most 2 blocks of any one session; in every row some shard holds exactly 2 blocks of some session. `block_index`: in each row, the slots of one session carry the indices 0 to 31, each once. `history_len`: some session has exactly 4096. `turn_len`: every value is at least 256 and some session has exactly 512. `step_size`: Positive. `decay_rate`: Positive.
All inputs are finite; a program needn't handle non-finite values.
Results may differ from the reference program's by a relative error of at most 0.008.
Values may be sent and summed in bfloat16 or wider, within the bound.
A program may use at most 64 MiB of HBM per device.

```python
import jax
import jax.numpy as jnp
from jax import lax

SSM_HEADS = 128
HEAD_P = 64
STATE = 256
GROUPS = 8
Q_HEADS = 64
KV_HEADS = 8
HEAD_DIM = 128
PAGE = 32
BLK = 128
REPLY_STEP_COUNT = 512
SESS = 32
SEGS = 4
HPAGES = 32
SLOTS = 1024
HIST = 4096
N_HEAD = 4


def route_tables(key):
    start_shift = jax.random.fold_in(key, 7)
    per_pair = HPAGES // SESS

    def one_segment(seg_key):
        key_order, key_delta, key_shuffle, key_place = jax.random.split(seg_key, 4)
        order = jax.random.permutation(key_order, SESS)
        delta = jax.random.randint(key_delta, (SESS // 2,), 0, per_pair + 1).at[0].set(per_pair)
        counts = jnp.full((SESS,), per_pair, jnp.int32).at[order[0::2]].add(delta).at[order[1::2]].add(-delta)
        source = jnp.arange(SESS, dtype=jnp.int32)
        table = counts[(source[:, None] - source[None, :]) % SESS]
        edges = jnp.cumsum(table, axis=1)
        slot_ids = jnp.arange(HPAGES, dtype=jnp.int32)
        owner_seq = jnp.sum((slot_ids[None, :, None] >= edges[:, None, :]).astype(jnp.int32), axis=2)
        shuffles = jax.vmap(lambda one_key: jax.random.permutation(one_key, HPAGES))(jax.random.split(key_shuffle, SESS))
        owners = jnp.zeros((SESS, HPAGES), jnp.int32).at[source[:, None], shuffles].set(owner_seq)
        flat = owners.reshape(-1)
        onehot = (flat[:, None] == source[None, :]).astype(jnp.int32)
        order_in = jnp.sum((jnp.cumsum(onehot, axis=0) - onehot) * onehot, axis=1)
        places = jax.vmap(lambda one_key: jax.random.permutation(one_key, HPAGES))(jax.random.split(key_place, SESS))
        return (flat.astype(jnp.int32), places[flat, order_in].astype(jnp.int32))
    return jax.vmap(one_segment)(jax.random.split(start_shift, SEGS))


def draw_block_owner(key, part):
    return route_tables(key)[0]


def draw_block_index(key, part):
    return route_tables(key)[1]


def draw_history_len(key, part):
    key_len, key_top = jax.random.split(jax.random.fold_in(key, 3))
    lengths = jax.random.randint(key_len, (SESS,), 1, HIST + 1)
    chosen = jax.random.randint(key_top, (), 0, SESS)
    return lengths.at[chosen].set(HIST).astype(jnp.int32)


def draw_turn_len(key, part):
    key_len, key_top = jax.random.split(jax.random.fold_in(key, 5))
    lengths = jax.random.randint(key_len, (SESS,), REPLY_STEP_COUNT // 2, REPLY_STEP_COUNT + 1)
    chosen = jax.random.randint(key_top, (), 0, SESS)
    return lengths.at[chosen].set(REPLY_STEP_COUNT).astype(jnp.int32)


def draw_step_size(key, part):
    key_base, key_spot, key_level = jax.random.split(jax.random.fold_in(key, 9), 3)
    shape = (SESS, SSM_HEADS, REPLY_STEP_COUNT)
    start_shift = jnp.exp(jax.random.uniform(key_base, shape, jnp.float32, jnp.log(0.005), jnp.log(0.02)))
    cell_places = jax.random.randint(key_spot, (SESS, 1, 3), 0, REPLY_STEP_COUNT)
    spike_spot = jnp.any(jnp.arange(REPLY_STEP_COUNT, dtype=jnp.int32)[None, None, :, None] == cell_places[:, :, None, :], axis=3)
    height_amount = jax.random.uniform(key_level, (SESS, 1, REPLY_STEP_COUNT), jnp.float32, 1.0, 2.0)
    return jnp.where(spike_spot, height_amount, start_shift).astype(jnp.float32)


def draw_decay_rate(key, part):
    key_kind, key_slow, key_fast = jax.random.split(jax.random.fold_in(key, 13), 3)
    quick = jax.random.randint(key_kind, (SSM_HEADS,), 0, 2) == 0
    slow = jax.random.uniform(key_slow, (SSM_HEADS,), jnp.float32, 15.0 / REPLY_STEP_COUNT, 75.0 / REPLY_STEP_COUNT)
    fast = jax.random.uniform(key_fast, (SSM_HEADS,), jnp.float32, 2.0, 4.0)
    return jnp.where(quick, fast, slow).astype(jnp.float32)


def attention_pair(key):
    key_query, key_kv = jax.random.split(jax.random.fold_in(key, 17))
    width = KV_HEADS * HEAD_DIM
    turn = jnp.clip(jax.random.normal(key_kv, (SESS, 2, REPLY_STEP_COUNT, width), jnp.float32), -6.0, 6.0)
    asked = jnp.clip(jax.random.normal(key_query, (SESS, REPLY_STEP_COUNT, Q_HEADS * HEAD_DIM), jnp.float32), -6.0, 6.0)
    return (asked, turn)


def draw_queries(key, part):
    return attention_pair(key)[0].astype(jnp.bfloat16)


def draw_turn_kv(key, part):
    return attention_pair(key)[1].astype(jnp.bfloat16)


def block_scale(key, dims, shards, low, largest):
    loudness, own = 1.0, jax.random.fold_in(key, 6)
    for dim, shards_of in shards:
        steps = jnp.exp(jax.random.uniform(jax.random.fold_in(own, dim), (shards_of,), jnp.float32, low / len(shards), largest / len(shards)))
        loudness = loudness * jnp.repeat(steps, dims[dim] // shards_of).reshape([-1 if axis == dim else 1 for axis in range(len(dims))])
    return loudness


def bell_draw(stream_key, shape, scale, reach, pieces=(), kind=jnp.bfloat16):
    gain = block_scale(stream_key, shape, pieces, -0.22, 0.18) if pieces else 1.0
    drawn = jax.random.normal(stream_key, shape, jnp.float32) * scale * gain
    return jnp.minimum(jnp.maximum(drawn, -reach), reach).astype(kind)


def setup_inputs(seed: int = 0) -> dict:
    key_of = jax.random.split(jax.random.key(seed), 15)
    kv_pool = bell_draw(key_of[0], (SEGS, SLOTS, 2, PAGE, KV_HEADS * HEAD_DIM), 1.0, 6.0, ((0, 4), (1, 32), (4, 4)))
    state_pool = bell_draw(key_of[1], (SLOTS, HEAD_P, N_HEAD * STATE), 0.1, 0.59765625, ((0, 32), (1, 4), (2, 4)))
    block_owner = draw_block_owner(jax.random.fold_in(key_of[14], 71), 0)
    block_index = draw_block_index(jax.random.fold_in(key_of[14], 71), 0)
    history_len = draw_history_len(jax.random.fold_in(key_of[14], 71), 0)
    turn_len = draw_turn_len(jax.random.fold_in(key_of[14], 71), 0)
    mixer_in = bell_draw(key_of[6], (SESS, SSM_HEADS, HEAD_P, REPLY_STEP_COUNT), 1.0, 6.0, ((0, 32), (1, 4), (2, 4)))
    input_proj = bell_draw(key_of[7], (SESS, GROUPS, STATE, REPLY_STEP_COUNT), 0.25, 1.5, ((0, 32), (1, 4)))
    output_proj = bell_draw(key_of[8], (SESS, GROUPS, STATE, REPLY_STEP_COUNT), 1.0, 6.0, ((0, 32), (1, 4)))
    step_size = draw_step_size(jax.random.fold_in(key_of[14], 71), 0)
    decay_rate = draw_decay_rate(jax.random.fold_in(key_of[14], 71), 0)
    bypass_factor = jnp.clip(0.5 + 1.0 * jax.random.uniform(key_of[11], (SSM_HEADS,), jnp.float32) ** block_scale(key_of[11], (SSM_HEADS,), ((0, 4),), -0.2, 0.2), 0.5, 1.5)
    queries = draw_queries(jax.random.fold_in(key_of[14], 71), 0)
    turn_kv = draw_turn_kv(jax.random.fold_in(key_of[14], 71), 0)
    return {"kv_pool": kv_pool, "state_pool": state_pool, "block_owner": block_owner, "block_index": block_index, "history_len": history_len, "turn_len": turn_len, "mixer_in": mixer_in, "input_proj": input_proj, "output_proj": output_proj, "step_size": step_size, "decay_rate": decay_rate, "bypass_factor": bypass_factor, "queries": queries, "turn_kv": turn_kv}


floor_score = -1e30


def spanned_ssd(values, input_proj, output_proj, step_sizes, rates, bypass_factor, start_state, valid_len):
    heads, channels, total = values.shape
    groups = input_proj.shape[0]
    per_group = heads // groups
    count = total // BLK
    positions = jnp.arange(total, dtype=jnp.int32)
    live = positions < valid_len
    step_sizes = jnp.where(live[None, :], step_sizes, jnp.float32(0.0))
    value_blocks = values.reshape(heads, channels, count, BLK).transpose(2, 0, 1, 3)
    input_blocks = input_proj.reshape(groups, -1, count, BLK).transpose(2, 0, 1, 3)
    output_blocks = output_proj.reshape(groups, -1, count, BLK).transpose(2, 0, 1, 3)
    step_blocks = step_sizes.reshape(heads, count, BLK).transpose(1, 0, 2)
    offsets = jnp.arange(BLK, dtype=jnp.int32)
    lower = offsets[:, None] >= offsets[None, :]
    exact = lax.Precision.HIGHEST

    def advance(carried, item):
        value_blk, input_blk, output_blk, step_blk = item
        value_blk = value_blk.astype(jnp.float32)
        input_blk = input_blk.astype(jnp.float32)
        output_blk = output_blk.astype(jnp.float32)
        running = jnp.cumsum(-rates[:, None] * step_blk, axis=1)
        pairs = jnp.einsum("gnt,gns->gts", output_blk, input_blk, precision=exact)
        pairs = jnp.repeat(pairs, per_group, axis=0)
        gaps = jnp.minimum(running[:, :, None] - running[:, None, :], 0.0)
        mixing = jnp.where(lower[None], jnp.exp(gaps), 0.0) * pairs * step_blk[:, None, :]
        result = jnp.einsum("hts,hps->hpt", mixing, value_blk, precision=exact)
        read_out = jnp.repeat(output_blk, per_group, axis=0)
        result = result + jnp.exp(running)[:, None, :] * jnp.einsum("hpn,hnt->hpt", carried, read_out, precision=exact)
        result = result + bypass_factor[:, None, None] * value_blk
        weights = jnp.exp(running[:, -1:] - running) * step_blk
        write_in = jnp.repeat(input_blk, per_group, axis=0)
        carried = jnp.exp(running[:, -1])[:, None, None] * carried + jnp.einsum("hps,hns->hpn", value_blk * weights[:, None, :], write_in, precision=exact)
        return carried, result

    final_state, results = lax.scan(advance, start_state, (value_blocks, input_blocks, output_blocks, step_blocks))
    results = results.transpose(1, 2, 0, 3).reshape(heads, channels, total)
    return jnp.where(live[None, None, :], results, 0.0), final_state


def session_attention(item):
    query_rows, history, turn_kv, history_len, turn_len = item
    per_group = Q_HEADS // KV_HEADS
    keys_all = jnp.concatenate([history[0], turn_kv[0]], axis=0)
    values_all = jnp.concatenate([history[1], turn_kv[1]], axis=0)
    positions = jnp.arange(HIST + REPLY_STEP_COUNT, dtype=jnp.int32)
    in_history = positions < HIST
    turn_index = jnp.arange(REPLY_STEP_COUNT, dtype=jnp.int32)
    seen_mask = jnp.where(in_history[None, :], (positions < history_len)[None, :], (positions - HIST)[None, :] <= turn_index[:, None])
    query_heads = query_rows.reshape(REPLY_STEP_COUNT, KV_HEADS, per_group, HEAD_DIM).transpose(1, 0, 2, 3)
    key_heads = keys_all.reshape(HIST + REPLY_STEP_COUNT, KV_HEADS, HEAD_DIM).transpose(1, 0, 2)
    value_heads = values_all.reshape(HIST + REPLY_STEP_COUNT, KV_HEADS, HEAD_DIM).transpose(1, 0, 2)
    score_scale = HEAD_DIM ** -0.5

    def one_group(group_member):
        query_grp, key_grp, value_grp = group_member
        scores = jnp.einsum("tqd,kd->tqk", query_grp.astype(jnp.float32), key_grp.astype(jnp.float32), precision=lax.Precision.HIGHEST) * score_scale
        mask = seen_mask[:, None, :]
        top = jnp.max(jnp.where(mask, scores, floor_score), axis=-1, keepdims=True)
        weights = jnp.where(mask, jnp.exp(scores - top), 0.0)
        totals = jnp.sum(weights, axis=-1, keepdims=True)
        rounded = lax.optimization_barrier(weights.astype(jnp.bfloat16)).astype(jnp.float32)
        mixed = jnp.einsum("tqk,kd->tqd", rounded, value_grp.astype(jnp.float32), precision=lax.Precision.HIGHEST)
        return mixed / totals

    outputs = lax.map(one_group, (query_heads, key_heads, value_heads))
    outputs = outputs.transpose(1, 0, 2, 3).reshape(REPLY_STEP_COUNT, Q_HEADS * HEAD_DIM)
    return jnp.where((turn_index < turn_len)[:, None], outputs, 0.0).astype(jnp.bfloat16)


def reference(kv_pool, state_pool, block_owner, block_index, history_len, turn_len, mixer_in, input_proj, output_proj, step_size, decay_rate, bypass_factor, queries, turn_kv):
    width = KV_HEADS * HEAD_DIM
    page_ids = (block_owner * (SEGS * HPAGES) + jnp.arange(SEGS, dtype=jnp.int32)[:, None] * HPAGES + block_index).reshape(-1).astype(jnp.int32)
    pages = jnp.zeros((SESS * SEGS * HPAGES, 2, PAGE, width), kv_pool.dtype).at[page_ids].set(kv_pool.reshape(SEGS * SLOTS, 2, PAGE, width))
    history = pages.reshape(SESS, SEGS * HPAGES, 2, PAGE, width).transpose(0, 2, 1, 3, 4).reshape(SESS, 2, HIST, width)
    seg_chan = HEAD_P // SEGS
    blocks = state_pool.reshape(SLOTS, SEGS, seg_chan, N_HEAD, STATE).transpose(1, 0, 2, 3, 4)

    def place(owners, entry_numbers, slabs):
        return jnp.zeros((SESS, HPAGES, seg_chan, N_HEAD, STATE), state_pool.dtype).at[owners, entry_numbers].set(slabs)

    saved = jax.vmap(place)(block_owner, block_index, blocks)
    saved = saved.transpose(1, 4, 2, 0, 3, 5).reshape(SESS, SSM_HEADS, HEAD_P, STATE).astype(jnp.float32)

    def mamba_one(item):
        values, inputs, outputs, steps, start, valid = item
        return spanned_ssd(values, inputs, outputs, steps, decay_rate, bypass_factor, start, valid)

    mixed, final = lax.map(mamba_one, (mixer_in, input_proj, output_proj, step_size, saved, turn_len))
    attended = lax.map(session_attention, (queries, history, turn_kv, history_len, turn_len))
    return mixed.astype(jnp.bfloat16), final, attended
```

```python
import functools

import jax
import jax.numpy as jnp
from jax import lax
from jax.experimental import pallas as pl
from jax.experimental.pallas import tpu as pltpu
from jax.sharding import PartitionSpec as P

BF = jnp.bfloat16
F32 = jnp.float32
I32 = jnp.int32
MESH = pl.DeviceIdType.MESH

POOL = 32
CTX = 4
PAGES = 32
PAGE = 32
HD = 128
QH = 8
KVH = 2
TOK = 128
TURN = 512
HEADS = 32
CH = 16
STATE = 256
GRP = 2
PER = 16
BLK = 128
HROWS = PAGES * PAGE
ROWS = HROWS + TOK
NEG = -1e30
SCALE = 1.4426950408889634 / (HD**0.5)


def nt(a, b):
    return lax.dot_general(a, b, (((1,), (1,)), ((), ())), preferred_element_type=F32)


def tn(a, b):
    return lax.dot_general(a, b, (((0,), (0,)), ((), ())), preferred_element_type=F32)


def build_tables(own, idx, me, tab_v):
    row = lax.broadcasted_iota(I32, (8, 128), 0)
    lane = lax.broadcasted_iota(I32, (8, 128), 1)
    quarter = lane // 32
    slot = lane % 32
    mine = own == me
    first = jnp.full((8, 128), 99, I32)
    for q in range(4):
        here = quarter == q
        low = jnp.min(jnp.where(here & mine, slot, 99), axis=1, keepdims=True)
        first = jnp.where(here, low, first)
    place = (row * 4 + quarter) * 2 + jnp.where(slot > first, 1, 0)
    place = jnp.where(mine, place, 0)
    block = lax.broadcasted_iota(I32, (PAGES, 128), 0)
    sums = jnp.zeros((PAGES, 128), I32)
    for j in range(PAGES):
        got = jnp.max(jnp.where(idx == j, place, 0), axis=0, keepdims=True)
        sums = jnp.where(block == j, got, sums)
    source = jnp.max(sums, axis=1, keepdims=True)
    local = (row == me // 4) & (quarter == me % 4)
    owners = jnp.sum(jnp.where(local, own + 1, 0), axis=0, keepdims=True) - 1
    wide = lax.broadcasted_iota(I32, (PAGES, 128), 1)
    match = owners == block
    low = jnp.min(jnp.where(match, wide % 32, 31), axis=1, keepdims=True)
    high = jnp.max(jnp.where(match, wide % 32, 0), axis=1, keepdims=True)
    tab_v[...] = jnp.where(wide == 0, low, jnp.where(wide == 1, high, source))


def mixer_local(tlen, rate_s, gain_s, x_v, b_v, c_v, step_v, cum_v, full_v, colw_v, y_v, s_v):
    head = lax.broadcasted_iota(I32, (HEADS, BLK), 0)
    rates = jnp.zeros((HEADS, BLK), F32)
    for h in range(HEADS):
        rates = jnp.where(head == h, rate_s[h], rates)
    up = (
        lax.broadcasted_iota(I32, (BLK, BLK), 0) <= lax.broadcasted_iota(I32, (BLK, BLK), 1)
    )
    ones = jnp.where(up, 1.0, 0.0).astype(F32)
    base = jnp.zeros((HEADS, 1), F32)
    when = lax.broadcasted_iota(I32, (HEADS, BLK), 1)
    for b in range(TURN // BLK):
        cols = slice(b * BLK, (b + 1) * BLK)
        step = jnp.where(when + b * BLK < tlen, step_v[:, cols], 0.0)
        step_v[:, cols] = step
        cum = lax.dot_general(
            -rates * step, ones, (((1,), (0,)), ((), ())),
            preferred_element_type=F32, precision=lax.Precision.HIGHEST,
        )
        cum_v[:, cols] = cum
        full_v[:, cols] = cum + base
        base = base + cum[:, BLK - 1 :]
        padded = jnp.concatenate([cum, jnp.zeros((BLK - HEADS, BLK), F32)], axis=0)
        colw_v[cols, :] = padded.T
    s_v[...] = jnp.zeros_like(s_v)

    def block(b, carry):
        at = pl.ds(pl.multiple_of(b * BLK, BLK), BLK)
        for g in range(GRP):
            bb = b_v[g, :, at]
            cb = c_v[g, :, at]
            pairs = jnp.where(up, tn(bb, cb), 0.0)
            state = s_v[g * PER : (g + 1) * PER].reshape(PER * CH, STATE)
            read = jnp.dot(state.astype(BF), cb, preferred_element_type=F32)
            cums = cum_v[g * PER : (g + 1) * PER, at]
            steps = step_v[g * PER : (g + 1) * PER, at]
            cols = colw_v[at, :]
            late = jnp.exp(cums[:, BLK - 1 :] - cums) * steps
            grow = jnp.exp(cums)
            written = []
            for i in range(PER):
                h = g * PER + i
                xh = x_v[h, :, at].astype(F32)
                gaps = jnp.minimum(cums[i : i + 1] - cols[:, h : h + 1], 0.0)
                mix = (pairs * jnp.exp(gaps)).astype(BF)
                xs = (xh * steps[i : i + 1]).astype(BF)
                y = jnp.dot(xs, mix, preferred_element_type=F32)
                y = y + grow[i : i + 1] * read[i * CH : (i + 1) * CH] + gain_s[h] * xh
                y_v[h, :, at] = y
                written.append((xh * late[i : i + 1]).astype(BF))
            added = nt(jnp.concatenate(written, axis=0), bb)
            for i in range(PER):
                h = g * PER + i
                s_v[h] = grow[i : i + 1, BLK - 1 :] * s_v[h] + added[i * CH : (i + 1) * CH]
        return carry

    lax.fori_loop(0, TURN // BLK, block, 0)


def mixer_saved(tlen, tab_s, saved_v, c_v, full_v, y_v, s_v, mix_o, next_o, s0_v):
    def pick(j, carry):
        s0_v[j] = saved_v[tab_s[j, 2]]
        return carry

    lax.fori_loop(0, HEADS, pick, 0)
    when = lax.broadcasted_iota(I32, (CH, TURN), 1)
    for g in range(GRP):
        start = s0_v[g * PER : (g + 1) * PER].reshape(PER * CH, STATE)
        read = jnp.dot(start, c_v[g], preferred_element_type=F32)
        for i in range(PER):
            h = g * PER + i
            grow = jnp.exp(full_v[h : h + 1, :])
            y = y_v[h] + grow * read[i * CH : (i + 1) * CH]
            mix_o[h] = jnp.where(when < tlen, y, 0.0).astype(BF)
            last = grow[:, TURN - 1 :]
            next_o[h] = last * s0_v[h].astype(F32) + s_v[h]


def attend(g, hlen, seg, q_all, k_v, v_v, o_send, l_send, send_part):
    key = lax.broadcasted_iota(I32, (1, HROWS), 1) + seg * HROWS
    seen = jnp.where(key < hlen, 0.0, NEG)
    half = QH // 2
    lane = lax.broadcasted_iota(I32, (TOK, 128), 1)

    def dest(k, carry):
        off = lax.rem(k + 1, CTX)
        c = lax.rem(seg + off, CTX)
        token = lax.broadcasted_iota(I32, (TOK, TOK), 0) + c * TOK
        fresh = lax.broadcasted_iota(I32, (TOK, TOK), 1) + seg * TOK
        turn = jnp.where(fresh <= token, 0.0, NEG)
        turn = jnp.concatenate([turn] * half, axis=0)
        keep = jnp.zeros((TOK, 128), F32)
        for part in range(2):
            first = g * QH + part * half
            q = jnp.concatenate(
                [q_all[c, :, (first + j) * HD : (first + j + 1) * HD] for j in range(half)], axis=0
            )
            s = nt(q, k_v[...]) * SCALE
            sh = s[:, :HROWS] + seen
            st = s[:, HROWS:] + turn
            top = jnp.maximum(
                jnp.max(sh, axis=1, keepdims=True), jnp.max(st, axis=1, keepdims=True)
            )
            ph = jnp.exp2(sh - top).astype(BF)
            pt = jnp.exp2(st - top).astype(BF)
            o = jnp.dot(ph, v_v[:HROWS], preferred_element_type=F32) + jnp.dot(
                pt, v_v[HROWS:], preferred_element_type=F32
            )
            total = o[:, HD:]
            out = (o[:, :HD] / total).astype(BF)
            logs = top + jnp.log2(total)
            for j in range(half):
                at = slice(j * TOK, (j + 1) * TOK)
                n = part * half + j
                o_send[g, k, :, n * HD : (n + 1) * HD] = out[at]
                keep = jnp.where(lane == n, logs[at], keep)
        l_send[g, k] = keep.T[:QH]

        @pl.when(k < CTX - 1)
        def _():
            send_part(g, k, off, c)

        return carry

    lax.fori_loop(0, CTX, dest, 0)


def merge(g, tlen, seg, o_send, l_send, o_recv, l_recv, att_o):
    logs = [l_recv[g, 0], l_recv[g, 1], l_recv[g, 2], l_send[g, CTX - 1]]
    top = functools.reduce(jnp.maximum, logs)
    parts = [jnp.exp2(l - top) for l in logs]
    whole = parts[0] + parts[1] + parts[2] + parts[3]
    shares = jnp.concatenate(
        [p / whole for p in parts] + [jnp.zeros((TOK - CTX * QH, 128), F32)], axis=0
    ).T
    live = lax.broadcasted_iota(I32, (TOK, HD), 0) + seg * TOK < tlen
    for j in range(QH):
        cols = slice(j * HD, (j + 1) * HD)
        out = jnp.zeros((TOK, HD), F32)
        for i in range(CTX):
            part = o_recv[g, i, :, cols] if i < CTX - 1 else o_send[g, CTX - 1, :, cols]
            n = i * QH + j
            out = out + shares[:, n : n + 1] * part.astype(F32)
        base = g * QH * HD
        att_o[:, base + j * HD : base + (j + 1) * HD] = jnp.where(live, out, 0.0).astype(BF)


def kernel(
    hlen_s, tlen_s, rate_s, gain_s, own_r, idx_r,
    kv_h, st_h, x_h, b_h, c_h, step_h, q_h, turn_h,
    mix_o, next_o, att_o,
    kv_v, st_v, x_v, b_v, c_v, step_v, turn_v, tab_v, tab_s,
    kv_send, kv_recv0, kv_recv1, st_send, st_recv, q_all,
    cum_v, full_v, colw_v, y_v, s_v, s0_v, k_v, v_v,
    o_send, l_send, o_recv, l_recv,
    in_sem, tab_sem, kv_ss, kv_rs, st_ss, st_rs, q_ss, q_rs, o_ss, o_rs, l_ss, l_rs,
):
    me = lax.axis_index("pool")
    seg = lax.axis_index("ctx")
    side = lax.axis_index("head")
    row, col = me // 8, me % 8
    hlen, tlen = hlen_s[0], tlen_s[0]
    kv_recv = (kv_recv0, kv_recv1)

    def peer(i):
        k = lax.rem(i * 11, POOL)
        return lax.rem(row + k // 8, 4) * 8 + lax.rem(col + lax.rem(k, 8), 8)

    loads = [
        pltpu.make_async_copy(src, dst, in_sem.at[i])
        for i, (src, dst) in enumerate(
            [
                (kv_h, kv_v), (st_h, st_v), (q_h, q_all.at[seg]), (x_h, x_v), (b_h, b_v),
                (c_h, c_v), (step_h, step_v), (turn_h, turn_v),
            ]
        )
    ]
    for load in loads:
        load.start()

    barrier = pltpu.get_barrier_semaphore()

    def greet(i, carry):
        pl.semaphore_signal(
            barrier, inc=1, device_id=(peer(i), seg, side), device_id_type=MESH
        )
        return carry

    lax.fori_loop(1, POOL, greet, 0)
    for off in range(1, CTX):
        pl.semaphore_signal(
            barrier, inc=1, device_id=(me, lax.rem(seg + off, CTX), side), device_id_type=MESH
        )
    build_tables(own_r[...], idx_r[...], me, tab_v)
    table = pltpu.make_async_copy(tab_v, tab_s, tab_sem)
    table.start()
    table.wait()
    loads[0].wait()
    pl.semaphore_wait(barrier, POOL - 1 + CTX - 1)

    def kv_copy(g, i):
        return pltpu.make_async_remote_copy(
            src_ref=kv_send.at[g, pl.ds(2 * i, 2)], dst_ref=kv_recv[g].at[pl.ds(2 * me, 2)],
            send_sem=kv_ss.at[g, i], recv_sem=kv_rs.at[g, i],
            device_id=(peer(i), seg, side), device_id_type=MESH,
        )

    def st_copy(i):
        return pltpu.make_async_remote_copy(
            src_ref=st_send.at[pl.ds(2 * i, 2)], dst_ref=st_recv.at[pl.ds(2 * me, 2)],
            send_sem=st_ss.at[i], recv_sem=st_rs.at[i],
            device_id=(peer(i), seg, side), device_id_type=MESH,
        )

    def q_copy(g, off):
        cols = pl.ds(g * QH * HD, QH * HD)
        return pltpu.make_async_remote_copy(
            src_ref=q_h.at[:, cols], dst_ref=q_all.at[seg, :, cols],
            send_sem=q_ss.at[g, off - 1], recv_sem=q_rs.at[g, off - 1],
            device_id=(me, lax.rem(seg + off, CTX), side), device_id_type=MESH,
        )

    for g in range(KVH):
        lanes = slice(g * HD, (g + 1) * HD)
        for r in range(2):
            kv_recv[g][2 * me + r] = kv_v[tab_s[me, r], :, :, lanes]

        def pack(i, carry):
            to = peer(i)
            for r in range(2):
                kv_send[g, 2 * i + r] = kv_v[tab_s[to, r], :, :, lanes]
            kv_copy(g, i).start()
            return carry

        lax.fori_loop(1, POOL, pack, 0)
        for off in range(1, CTX):
            q_copy(g, off).start()
    loads[1].wait()
    for r in range(2):
        st_recv[2 * me + r] = st_v[tab_s[me, r]]

    def pack_state(i, carry):
        to = peer(i)
        for r in range(2):
            st_send[2 * i + r] = st_v[tab_s[to, r]]
        st_copy(i).start()
        return carry

    lax.fori_loop(1, POOL, pack_state, 0)

    for load in loads[2:]:
        load.wait()
    mixer_local(tlen, rate_s, gain_s, x_v, b_v, c_v, step_v, cum_v, full_v, colw_v, y_v, s_v)

    v_v[:, HD:] = jnp.ones((ROWS, HD), BF)

    def o_copy(g, k, off, c):
        return pltpu.make_async_remote_copy(
            src_ref=o_send.at[g, k], dst_ref=o_recv.at[g, k],
            send_sem=o_ss.at[g, k], recv_sem=o_rs.at[g, k],
            device_id=(me, c, side), device_id_type=MESH,
        )

    def l_copy(g, k, off, c):
        return pltpu.make_async_remote_copy(
            src_ref=l_send.at[g, k], dst_ref=l_recv.at[g, k],
            send_sem=l_ss.at[g, k], recv_sem=l_rs.at[g, k],
            device_id=(me, c, side), device_id_type=MESH,
        )

    def send_part(g, k, off, c):
        o_copy(g, k, off, c).start()
        l_copy(g, k, off, c).start()

    for g in range(KVH):
        lanes = slice(g * HD, (g + 1) * HD)

        def arrive(i, carry):
            kv_copy(g, i).wait_recv()
            return carry

        lax.fori_loop(1, POOL, arrive, 0)

        def place(j, carry):
            page = kv_recv[g][tab_s[j, 2]]
            at = pl.ds(pl.multiple_of(j * PAGE, PAGE), PAGE)
            k_v[at, :] = page[0]
            v_v[at, :HD] = page[1]
            return carry

        lax.fori_loop(0, PAGES, place, 0)
        k_v[HROWS:, :] = turn_v[0, :, lanes]
        v_v[HROWS:, :HD] = turn_v[1, :, lanes]
        for off in range(1, CTX):
            q_copy(g, off).wait_recv()
        attend(g, hlen, seg, q_all, k_v, v_v, o_send, l_send, send_part)

    def state_arrives(i, carry):
        st_copy(i).wait_recv()
        return carry

    lax.fori_loop(1, POOL, state_arrives, 0)
    mixer_saved(tlen, tab_s, st_recv, c_v, full_v, y_v, s_v, mix_o, next_o, s0_v)

    for g in range(KVH):
        for k in range(CTX - 1):
            off = k + 1
            c = lax.rem(seg + off, CTX)
            o_copy(g, k, off, c).wait_recv()
            l_copy(g, k, off, c).wait_recv()
        merge(g, tlen, seg, o_send, l_send, o_recv, l_recv, att_o)

    def drain(i, carry):
        for g in range(KVH):
            kv_copy(g, i).wait_send()
        st_copy(i).wait_send()
        return carry

    lax.fori_loop(1, POOL, drain, 0)
    for g in range(KVH):
        for k in range(CTX - 1):
            off = k + 1
            c = lax.rem(seg + off, CTX)
            q_copy(g, off).wait_send()
            o_copy(g, k, off, c).wait_send()
            l_copy(g, k, off, c).wait_send()


def local(
    kv_pool, state_pool, block_owner, block_index, history_len, turn_len, mixer_in, input_proj,
    output_proj, step_size, decay_rate, bypass_factor, queries, turn_kv,
):
    hbm = pl.BlockSpec(memory_space=pl.ANY)
    vmem = pl.BlockSpec(memory_space=pltpu.VMEM)
    smem = pl.BlockSpec(memory_space=pltpu.SMEM)
    dma = pltpu.SemaphoreType.DMA
    mixed, final, attended = pl.pallas_call(
        kernel,
        out_shape=(
            jax.ShapeDtypeStruct((HEADS, CH, TURN), BF),
            jax.ShapeDtypeStruct((HEADS, CH, STATE), F32),
            jax.ShapeDtypeStruct((TOK, KVH * QH * HD), BF),
        ),
        in_specs=[smem] * 4 + [vmem] * 2 + [hbm] * 8,
        out_specs=(vmem, vmem, vmem),
        scratch_shapes=[
            pltpu.VMEM((PAGES, 2, PAGE, KVH * HD), BF),
            pltpu.VMEM((PAGES, CH, STATE), BF),
            pltpu.VMEM((HEADS, CH, TURN), BF),
            pltpu.VMEM((GRP, STATE, TURN), BF),
            pltpu.VMEM((GRP, STATE, TURN), BF),
            pltpu.VMEM((HEADS, TURN), F32),
            pltpu.VMEM((2, TOK, KVH * HD), BF),
            pltpu.VMEM((PAGES, 128), I32),
            pltpu.SMEM((PAGES, 128), I32),
            pltpu.VMEM((KVH, 2 * POOL, 2, PAGE, HD), BF),
            pltpu.VMEM((2 * POOL, 2, PAGE, HD), BF),
            pltpu.VMEM((2 * POOL, 2, PAGE, HD), BF),
            pltpu.VMEM((2 * POOL, CH, STATE), BF),
            pltpu.VMEM((2 * POOL, CH, STATE), BF),
            pltpu.VMEM((CTX, TOK, KVH * QH * HD), BF),
            pltpu.VMEM((HEADS, TURN), F32),
            pltpu.VMEM((HEADS, TURN), F32),
            pltpu.VMEM((TURN, 128), F32),
            pltpu.VMEM((HEADS, CH, TURN), F32),
            pltpu.VMEM((HEADS, CH, STATE), F32),
            pltpu.VMEM((HEADS, CH, STATE), BF),
            pltpu.VMEM((ROWS, HD), BF),
            pltpu.VMEM((ROWS, 2 * HD), BF),
            pltpu.VMEM((KVH, CTX, TOK, QH * HD), BF),
            pltpu.VMEM((KVH, CTX, QH, TOK), F32),
            pltpu.VMEM((KVH, CTX - 1, TOK, QH * HD), BF),
            pltpu.VMEM((KVH, CTX - 1, QH, TOK), F32),
            dma((8,)), dma(()),
            dma((KVH, POOL)), dma((KVH, POOL)), dma((POOL,)), dma((POOL,)),
            dma((KVH, CTX - 1)), dma((KVH, CTX - 1)), dma((KVH, CTX - 1)), dma((KVH, CTX - 1)),
            dma((KVH, CTX - 1)), dma((KVH, CTX - 1)),
        ],
        compiler_params=pltpu.CompilerParams(
            collective_id=0, has_side_effects=True, vmem_limit_bytes=56 << 20
        ),
        name="resume",
    )(
        history_len, turn_len, decay_rate, bypass_factor,
        block_owner.reshape(8, 128), block_index.reshape(8, 128),
        kv_pool[0], state_pool, mixer_in[0], input_proj[0], output_proj[0], step_size[0],
        queries[0], turn_kv[0],
    )
    return mixed[None], final[None], attended[None]


def solution(mesh):
    return jax.shard_map(
        local,
        mesh=mesh,
        in_specs=(
            P("ctx", "pool", None, None, "head"),
            P("pool", "ctx", "head"),
            P("ctx", None),
            P("ctx", None),
            P("pool"),
            P("pool"),
            P("pool", "head", "ctx", None),
            P("pool", "head", None, None),
            P("pool", "head", None, None),
            P("pool", "head", None),
            P("head"),
            P("head"),
            P("pool", "ctx", "head"),
            P("pool", None, "ctx", "head"),
        ),
        out_specs=(
            P("pool", "head", "ctx", None),
            P("pool", "head", "ctx", None),
            P("pool", "ctx", "head"),
        ),
        check_vma=False,
    )
```

```python
import functools

import jax
import jax.numpy as jnp
from jax import lax
from jax.experimental import pallas as pl
from jax.experimental.pallas import tpu as pltpu
from jax.sharding import PartitionSpec as P

BF = jnp.bfloat16
F32 = jnp.float32
I32 = jnp.int32
MESH = pl.DeviceIdType.MESH

POOL = 32
CTX = 4
PAGES = 32
PAGE = 32
HD = 128
QH = 8
KVH = 2
TOK = 128
TURN = 512
HEADS = 32
CH = 16
STATE = 256
GRP = 2
PER = 16
BLK = 128
HROWS = PAGES * PAGE
ROWS = HROWS + TOK
NEG = -1e30
SCALE = 1.4426950408889634 / (HD**0.5)


def nt(a, b):
    return lax.dot_general(a, b, (((1,), (1,)), ((), ())), preferred_element_type=F32)


def tn(a, b):
    return lax.dot_general(a, b, (((0,), (0,)), ((), ())), preferred_element_type=F32)


def build_tables(own, idx, me, tab_v):
    row = lax.broadcasted_iota(I32, (8, 128), 0)
    lane = lax.broadcasted_iota(I32, (8, 128), 1)
    quarter = lane // 32
    slot = lane % 32
    mine = own == me
    first = jnp.full((8, 128), 99, I32)
    for q in range(4):
        here = quarter == q
        low = jnp.min(jnp.where(here & mine, slot, 99), axis=1, keepdims=True)
        first = jnp.where(here, low, first)
    place = (row * 4 + quarter) * 2 + jnp.where(slot > first, 1, 0)
    place = jnp.where(mine, place, 0)
    block = lax.broadcasted_iota(I32, (PAGES, 128), 0)
    sums = jnp.zeros((PAGES, 128), I32)
    for j in range(PAGES):
        got = jnp.max(jnp.where(idx == j, place, 0), axis=0, keepdims=True)
        sums = jnp.where(block == j, got, sums)
    source = jnp.max(sums, axis=1, keepdims=True)
    local = (row == me // 4) & (quarter == me % 4)
    owners = jnp.sum(jnp.where(local, own + 1, 0), axis=0, keepdims=True) - 1
    wide = lax.broadcasted_iota(I32, (PAGES, 128), 1)
    match = owners == block
    low = jnp.min(jnp.where(match, wide % 32, 31), axis=1, keepdims=True)
    high = jnp.max(jnp.where(match, wide % 32, 0), axis=1, keepdims=True)
    tab_v[...] = jnp.where(wide == 0, low, jnp.where(wide == 1, high, source))


def mixer_local(tlen, rate_s, gain_s, x_v, b_v, c_v, step_v, cum_v, full_v, colw_v, y_v, s_v):
    head = lax.broadcasted_iota(I32, (HEADS, BLK), 0)
    rates = jnp.zeros((HEADS, BLK), F32)
    for h in range(HEADS):
        rates = jnp.where(head == h, rate_s[h], rates)
    up = (
        lax.broadcasted_iota(I32, (BLK, BLK), 0) <= lax.broadcasted_iota(I32, (BLK, BLK), 1)
    )
    ones = jnp.where(up, 1.0, 0.0).astype(F32)
    base = jnp.zeros((HEADS, 1), F32)
    when = lax.broadcasted_iota(I32, (HEADS, BLK), 1)
    for b in range(TURN // BLK):
        cols = slice(b * BLK, (b + 1) * BLK)
        step = jnp.where(when + b * BLK < tlen, step_v[:, cols], 0.0)
        step_v[:, cols] = step
        cum = lax.dot_general(
            -rates * step, ones, (((1,), (0,)), ((), ())),
            preferred_element_type=F32, precision=lax.Precision.HIGHEST,
        )
        cum_v[:, cols] = cum
        full_v[:, cols] = cum + base
        base = base + cum[:, BLK - 1 :]
        padded = jnp.concatenate([cum, jnp.zeros((BLK - HEADS, BLK), F32)], axis=0)
        colw_v[cols, :] = padded.T
    s_v[...] = jnp.zeros_like(s_v)

    def block(b, carry):
        at = pl.ds(pl.multiple_of(b * BLK, BLK), BLK)
        for g in range(GRP):
            bb = b_v[g, :, at]
            cb = c_v[g, :, at]
            pairs = jnp.where(up, tn(bb, cb), 0.0)
            state = s_v[g * PER : (g + 1) * PER].reshape(PER * CH, STATE)
            read = jnp.dot(state.astype(BF), cb, preferred_element_type=F32)
            cums = cum_v[g * PER : (g + 1) * PER, at]
            steps = step_v[g * PER : (g + 1) * PER, at]
            cols = colw_v[at, :]
            late = jnp.exp(cums[:, BLK - 1 :] - cums) * steps
            grow = jnp.exp(cums)
            written = []
            for i in range(PER):
                h = g * PER + i
                xh = x_v[h, :, at].astype(F32)
                gaps = jnp.minimum(cums[i : i + 1] - cols[:, h : h + 1], 0.0)
                mix = (pairs * jnp.exp(gaps)).astype(BF)
                xs = (xh * steps[i : i + 1]).astype(BF)
                y = jnp.dot(xs, mix, preferred_element_type=F32)
                y = y + grow[i : i + 1] * read[i * CH : (i + 1) * CH] + gain_s[h] * xh
                y_v[h, :, at] = y
                written.append((xh * late[i : i + 1]).astype(BF))
            added = nt(jnp.concatenate(written, axis=0), bb)
            for i in range(PER):
                h = g * PER + i
                s_v[h] = grow[i : i + 1, BLK - 1 :] * s_v[h] + added[i * CH : (i + 1) * CH]
        return carry

    lax.fori_loop(0, TURN // BLK, block, 0)


def mixer_saved(tlen, tab_s, saved_v, c_v, full_v, y_v, s_v, mix_o, next_o, s0_v):
    def pick(j, carry):
        s0_v[j] = saved_v[tab_s[j, 2]]
        return carry

    lax.fori_loop(0, HEADS, pick, 0)
    when = lax.broadcasted_iota(I32, (CH, TURN), 1)
    for g in range(GRP):
        start = s0_v[g * PER : (g + 1) * PER].reshape(PER * CH, STATE)
        read = jnp.dot(start, c_v[g], preferred_element_type=F32)
        for i in range(PER):
            h = g * PER + i
            grow = jnp.exp(full_v[h : h + 1, :])
            y = y_v[h] + grow * read[i * CH : (i + 1) * CH]
            mix_o[h] = jnp.where(when < tlen, y, 0.0).astype(BF)
            last = grow[:, TURN - 1 :]
            next_o[h] = last * s0_v[h].astype(F32) + s_v[h]


def attend(g, hlen, seg, q_all, k_v, v_v, o_send, l_send, send_part):
    key = lax.broadcasted_iota(I32, (1, HROWS), 1) + seg * HROWS
    seen = jnp.where(key < hlen, 0.0, NEG)
    half = QH // 2
    lane = lax.broadcasted_iota(I32, (TOK, 128), 1)

    def dest(k, carry):
        off = lax.rem(k + 1, CTX)
        c = lax.rem(seg + off, CTX)
        token = lax.broadcasted_iota(I32, (TOK, TOK), 0) + c * TOK
        fresh = lax.broadcasted_iota(I32, (TOK, TOK), 1) + seg * TOK
        turn = jnp.where(fresh <= token, 0.0, NEG)
        turn = jnp.concatenate([turn] * half, axis=0)
        keep = jnp.zeros((TOK, 128), F32)
        for part in range(2):
            first = g * QH + part * half
            q = jnp.concatenate(
                [q_all[c, :, (first + j) * HD : (first + j + 1) * HD] for j in range(half)], axis=0
            )
            s = nt(q, k_v[...]) * SCALE
            sh = s[:, :HROWS] + seen
            st = s[:, HROWS:] + turn
            top = jnp.maximum(
                jnp.max(sh, axis=1, keepdims=True), jnp.max(st, axis=1, keepdims=True)
            )
            ph = jnp.exp2(sh - top).astype(BF)
            pt = jnp.exp2(st - top).astype(BF)
            o = jnp.dot(ph, v_v[:HROWS], preferred_element_type=F32) + jnp.dot(
                pt, v_v[HROWS:], preferred_element_type=F32
            )
            total = o[:, HD:]
            out = (o[:, :HD] / total).astype(BF)
            logs = top + jnp.log2(total)
            for j in range(half):
                at = slice(j * TOK, (j + 1) * TOK)
                n = part * half + j
                o_send[g, k, :, n * HD : (n + 1) * HD] = out[at]
                keep = jnp.where(lane == n, logs[at], keep)
        l_send[g, k] = keep.T[:QH]

        @pl.when(k < CTX - 1)
        def _():
            send_part(g, k, off, c)

        return carry

    lax.fori_loop(0, CTX, dest, 0)


def merge(g, tlen, seg, o_send, l_send, o_recv, l_recv, att_o):
    logs = [l_recv[g, 0], l_recv[g, 1], l_recv[g, 2], l_send[g, CTX - 1]]
    top = functools.reduce(jnp.maximum, logs)
    parts = [jnp.exp2(l - top) for l in logs]
    whole = parts[0] + parts[1] + parts[2] + parts[3]
    shares = jnp.concatenate(
        [p / whole for p in parts] + [jnp.zeros((TOK - CTX * QH, 128), F32)], axis=0
    ).T
    live = lax.broadcasted_iota(I32, (TOK, HD), 0) + seg * TOK < tlen
    for j in range(QH):
        cols = slice(j * HD, (j + 1) * HD)
        out = jnp.zeros((TOK, HD), F32)
        for i in range(CTX):
            part = o_recv[g, i, :, cols] if i < CTX - 1 else o_send[g, CTX - 1, :, cols]
            n = i * QH + j
            out = out + shares[:, n : n + 1] * part.astype(F32)
        base = g * QH * HD
        att_o[:, base + j * HD : base + (j + 1) * HD] = jnp.where(live, out, 0.0).astype(BF)


def kernel(
    rate_s, gain_s, own_r, idx_r, hlen_h, tlen_h,
    kv_h, st_h, x_h, b_h, c_h, step_h, q_h, turn_h,
    mix_o, next_o, att_o,
    hlen_s, tlen_s, kv_v, st_v, x_v, b_v, c_v, step_v, turn_v, tab_v, tab_s,
    kv_send, kv_recv0, kv_recv1, st_send, st_recv, q_all,
    cum_v, full_v, colw_v, y_v, s_v, s0_v, k_v, v_v,
    o_send, l_send, o_recv, l_recv,
    in_sem, tab_sem, kv_ss, kv_rs, st_ss, st_rs, q_ss, q_rs, o_ss, o_rs, l_ss, l_rs,
):
    me = lax.axis_index("pool")
    seg = lax.axis_index("ctx")
    side = lax.axis_index("head")
    row, col = me // 8, me % 8
    kv_recv = (kv_recv0, kv_recv1)

    def peer(i):
        k = lax.rem(i * jnp.where(side % 2 == 0, 11, 21), POOL)
        return lax.rem(row + k // 8, 4) * 8 + lax.rem(col + lax.rem(k, 8), 8)

    barrier = pltpu.get_barrier_semaphore()

    def greet(i, carry):
        pl.semaphore_signal(
            barrier, inc=1, device_id=(peer(i), seg, side), device_id_type=MESH
        )
        return carry

    lax.fori_loop(1, POOL, greet, 0)
    for off in range(1, CTX):
        pl.semaphore_signal(
            barrier, inc=1, device_id=(me, lax.rem(seg + off, CTX), side), device_id_type=MESH
        )

    loads = [
        pltpu.make_async_copy(src, dst, in_sem.at[i])
        for i, (src, dst) in enumerate(
            [
                (kv_h, kv_v), (st_h, st_v), (q_h, q_all.at[seg]), (x_h, x_v), (b_h, b_v),
                (c_h, c_v), (step_h, step_v), (turn_h, turn_v), (hlen_h, hlen_s), (tlen_h, tlen_s),
            ]
        )
    ]
    for load in loads:
        load.start()
    build_tables(own_r[...], idx_r[...], me, tab_v)
    table = pltpu.make_async_copy(tab_v, tab_s, tab_sem)
    table.start()

    def kv_copy(g, i):
        return pltpu.make_async_remote_copy(
            src_ref=kv_send.at[g, pl.ds(2 * i, 2)], dst_ref=kv_recv[g].at[pl.ds(2 * me, 2)],
            send_sem=kv_ss.at[g, i], recv_sem=kv_rs.at[g, i],
            device_id=(peer(i), seg, side), device_id_type=MESH,
        )

    def st_copy(i):
        return pltpu.make_async_remote_copy(
            src_ref=st_send.at[pl.ds(2 * i, 2)], dst_ref=st_recv.at[pl.ds(2 * me, 2)],
            send_sem=st_ss.at[i], recv_sem=st_rs.at[i],
            device_id=(peer(i), seg, side), device_id_type=MESH,
        )

    def q_copy(g, off):
        cols = pl.ds(g * QH * HD, QH * HD)
        return pltpu.make_async_remote_copy(
            src_ref=q_h.at[:, cols], dst_ref=q_all.at[seg, :, cols],
            send_sem=q_ss.at[g, off - 1], recv_sem=q_rs.at[g, off - 1],
            device_id=(me, lax.rem(seg + off, CTX), side), device_id_type=MESH,
        )

    def o_copy(g, k, c):
        return pltpu.make_async_remote_copy(
            src_ref=o_send.at[g, k], dst_ref=o_recv.at[g, k],
            send_sem=o_ss.at[g, k], recv_sem=o_rs.at[g, k],
            device_id=(me, c, side), device_id_type=MESH,
        )

    def l_copy(g, k, c):
        return pltpu.make_async_remote_copy(
            src_ref=l_send.at[g, k], dst_ref=l_recv.at[g, k],
            send_sem=l_ss.at[g, k], recv_sem=l_rs.at[g, k],
            device_id=(me, c, side), device_id_type=MESH,
        )

    def send_part(g, k, off, c):
        o_copy(g, k, c).start()
        l_copy(g, k, c).start()

    def pack_kv(g):
        lanes = slice(g * HD, (g + 1) * HD)

        def pack(i, carry):
            to = peer(i)
            for r in range(2):
                kv_send[g, 2 * i + r] = kv_v[tab_s[to, r], :, :, lanes]
            return carry

        lax.fori_loop(1, POOL, pack, 0)
        for r in range(2):
            kv_recv[g][2 * me + r] = kv_v[tab_s[me, r], :, :, lanes]

    def each(body, first=1, last=POOL):
        def step(i, carry):
            body(i)
            return carry

        lax.fori_loop(first, last, step, 0)

    def arrive_kv(g):
        lanes = slice(g * HD, (g + 1) * HD)
        if g == 0:
            each(lambda i: kv_copy(g, i).wait_recv())

        def place(j):
            page = kv_recv[g][tab_s[j, 2]]
            at = pl.ds(pl.multiple_of(j * PAGE, PAGE), PAGE)
            k_v[at, :] = page[0]
            v_v[at, :HD] = page[1]

        each(place, 0, PAGES)
        k_v[HROWS:, :] = turn_v[0, :, lanes]
        v_v[HROWS:, :HD] = turn_v[1, :, lanes]
        for off in range(1, CTX):
            q_copy(g, off).wait_recv()

    def join(g):
        for k in range(CTX - 1):
            c = lax.rem(seg + k + 1, CTX)
            o_copy(g, k, c).wait_recv()
            l_copy(g, k, c).wait_recv()
        merge(g, tlen_s[0], seg, o_send, l_send, o_recv, l_recv, att_o)

    table.wait()
    loads[0].wait()
    pack_kv(0)
    pl.semaphore_wait(barrier, POOL - 1 + CTX - 1)
    each(lambda i: kv_copy(0, i).start())
    for off in range(1, CTX):
        q_copy(0, off).start()
    for off in range(1, CTX):
        q_copy(1, off).start()
    pack_kv(1)
    loads[1].wait()
    for r in range(2):
        st_recv[2 * me + r] = st_v[tab_s[me, r]]

    def pack_state(i):
        to = peer(i)
        for r in range(2):
            st_send[2 * i + r] = st_v[tab_s[to, r]]

    each(lambda i: kv_copy(1, i).start())
    each(pack_state)
    for load in loads[2:]:
        load.wait()
    hlen, tlen = hlen_s[0], tlen_s[0]
    mixer_local(tlen, rate_s, gain_s, x_v, b_v, c_v, step_v, cum_v, full_v, colw_v, y_v, s_v)
    v_v[:, HD:] = jnp.ones((ROWS, HD), BF)

    def second(i):
        kv_copy(0, i).wait_send()
        kv_copy(1, i).start()

    arrive_kv(0)
    attend(0, hlen, seg, q_all, k_v, v_v, o_send, l_send, send_part)

    def third(i):
        kv_copy(1, i).wait_send()
        st_copy(i).start()

    each(lambda i: kv_copy(1, i).wait_recv())
    each(third)
    arrive_kv(1)
    attend(1, hlen, seg, q_all, k_v, v_v, o_send, l_send, send_part)
    join(0)
    each(lambda i: st_copy(i).wait_recv())
    mixer_saved(tlen, tab_s, st_recv, c_v, full_v, y_v, s_v, mix_o, next_o, s0_v)
    join(1)

    each(lambda i: st_copy(i).wait_send())
    each(lambda i: kv_copy(0, i).wait_send())
    for g in range(KVH):
        for k in range(CTX - 1):
            c = lax.rem(seg + k + 1, CTX)
            q_copy(g, k + 1).wait_send()
            o_copy(g, k, c).wait_send()
            l_copy(g, k, c).wait_send()


def hand_over(a, b, c, x, y, z, u, v, w, sem):
    trips = [(a, u, x), (b, v, y), (c, w, z)]
    there = [pltpu.make_async_copy(src, mid, sem.at[0, i]) for i, (src, mid, _) in enumerate(trips)]
    back = [pltpu.make_async_copy(mid, dst, sem.at[1, i]) for i, (_, mid, dst) in enumerate(trips)]
    for copy in there:
        copy.start()
    for first, then in zip(there, back):
        first.wait()
        then.start()
    for copy in back:
        copy.wait()


def local(
    kv_pool, state_pool, block_owner, block_index, history_len, turn_len, mixer_in, input_proj,
    output_proj, step_size, decay_rate, bypass_factor, queries, turn_kv,
):
    hbm = pl.BlockSpec(memory_space=pl.ANY)
    vmem = pl.BlockSpec(memory_space=pltpu.VMEM)
    smem = pl.BlockSpec(memory_space=pltpu.SMEM)
    dma = pltpu.SemaphoreType.DMA
    outs = (
        jax.ShapeDtypeStruct((HEADS, CH, TURN), BF),
        jax.ShapeDtypeStruct((HEADS, CH, STATE), F32),
        jax.ShapeDtypeStruct((TOK, KVH * QH * HD), BF),
    )
    results = pl.pallas_call(
        kernel,
        out_shape=outs,
        in_specs=[smem] * 2 + [vmem] * 2 + [pl.BlockSpec(memory_space=pltpu.HBM)] * 2 + [hbm] * 8,
        out_specs=(vmem, vmem, vmem),
        scratch_shapes=[
            pltpu.SMEM((1,), I32),
            pltpu.SMEM((1,), I32),
            pltpu.VMEM((PAGES, 2, PAGE, KVH * HD), BF),
            pltpu.VMEM((PAGES, CH, STATE), BF),
            pltpu.VMEM((HEADS, CH, TURN), BF),
            pltpu.VMEM((GRP, STATE, TURN), BF),
            pltpu.VMEM((GRP, STATE, TURN), BF),
            pltpu.VMEM((HEADS, TURN), F32),
            pltpu.VMEM((2, TOK, KVH * HD), BF),
            pltpu.VMEM((PAGES, 128), I32),
            pltpu.SMEM((PAGES, 128), I32),
            pltpu.VMEM((KVH, 2 * POOL, 2, PAGE, HD), BF),
            pltpu.VMEM((2 * POOL, 2, PAGE, HD), BF),
            pltpu.VMEM((2 * POOL, 2, PAGE, HD), BF),
            pltpu.VMEM((2 * POOL, CH, STATE), BF),
            pltpu.VMEM((2 * POOL, CH, STATE), BF),
            pltpu.VMEM((CTX, TOK, KVH * QH * HD), BF),
            pltpu.VMEM((HEADS, TURN), F32),
            pltpu.VMEM((HEADS, TURN), F32),
            pltpu.VMEM((TURN, 128), F32),
            pltpu.VMEM((HEADS, CH, TURN), F32),
            pltpu.VMEM((HEADS, CH, STATE), F32),
            pltpu.VMEM((HEADS, CH, STATE), BF),
            pltpu.VMEM((ROWS, HD), BF),
            pltpu.VMEM((ROWS, 2 * HD), BF),
            pltpu.VMEM((KVH, CTX, TOK, QH * HD), BF),
            pltpu.VMEM((KVH, CTX, QH, TOK), F32),
            pltpu.VMEM((KVH, CTX - 1, TOK, QH * HD), BF),
            pltpu.VMEM((KVH, CTX - 1, QH, TOK), F32),
            dma((10,)), dma(()),
            dma((KVH, POOL)), dma((KVH, POOL)), dma((POOL,)), dma((POOL,)),
            dma((KVH, CTX - 1)), dma((KVH, CTX - 1)), dma((KVH, CTX - 1)), dma((KVH, CTX - 1)),
            dma((KVH, CTX - 1)), dma((KVH, CTX - 1)),
        ],
        compiler_params=pltpu.CompilerParams(
            collective_id=0, has_side_effects=True, vmem_limit_bytes=56 << 20
        ),
        name="resume",
    )(
        decay_rate, bypass_factor,
        block_owner.reshape(8, 128), block_index.reshape(8, 128), history_len, turn_len,
        kv_pool[0], state_pool, mixer_in[0], input_proj[0], output_proj[0], step_size[0],
        queries[0], turn_kv[0],
    )
    mixed, final, attended = pl.pallas_call(
        hand_over,
        out_shape=outs,
        in_specs=[hbm] * 3,
        out_specs=(hbm,) * 3,
        scratch_shapes=[pltpu.VMEM(o.shape, o.dtype) for o in outs] + [dma((2, 3))],
        name="hand_over",
    )(*results)
    return mixed[None], final[None], attended[None]


def solution(mesh):
    return jax.shard_map(
        local,
        mesh=mesh,
        in_specs=(
            P("ctx", "pool", None, None, "head"),
            P("pool", "ctx", "head"),
            P("ctx", None),
            P("ctx", None),
            P("pool"),
            P("pool"),
            P("pool", "head", "ctx", None),
            P("pool", "head", None, None),
            P("pool", "head", None, None),
            P("pool", "head", None),
            P("head"),
            P("head"),
            P("pool", "ctx", "head"),
            P("pool", None, "ctx", "head"),
        ),
        out_specs=(
            P("pool", "head", "ctx", None),
            P("pool", "head", "ctx", None),
            P("pool", "ctx", "head"),
        ),
        check_vma=False,
    )
```

```python
import functools

import jax
import jax.numpy as jnp
from jax import lax
from jax.experimental import pallas as pl
from jax.experimental.pallas import tpu as pltpu
from jax.sharding import PartitionSpec as P

BF = jnp.bfloat16
F32 = jnp.float32
I32 = jnp.int32
MESH = pl.DeviceIdType.MESH

POOL = 32
CTX = 4
PAGES = 32
PAGE = 32
HD = 128
QH = 8
KVH = 2
TOK = 128
TURN = 512
HEADS = 32
CH = 16
STATE = 256
GRP = 2
PER = 16
BLK = 128
HROWS = PAGES * PAGE
ROWS = HROWS + TOK
NEG = -1e30
SCALE = 1.4426950408889634 / (HD**0.5)


def nt(a, b):
    return lax.dot_general(a, b, (((1,), (1,)), ((), ())), preferred_element_type=F32)


def tn(a, b):
    return lax.dot_general(a, b, (((0,), (0,)), ((), ())), preferred_element_type=F32)


def build_tables(own, idx, me, tab_v):
    row = lax.broadcasted_iota(I32, (8, 128), 0)
    lane = lax.broadcasted_iota(I32, (8, 128), 1)
    quarter = lane // 32
    slot = lane % 32
    mine = own == me
    first = jnp.full((8, 128), 99, I32)
    for q in range(4):
        here = quarter == q
        low = jnp.min(jnp.where(here & mine, slot, 99), axis=1, keepdims=True)
        first = jnp.where(here, low, first)
    place = (row * 4 + quarter) * 2 + jnp.where(slot > first, 1, 0)
    place = jnp.where(mine, place, 0)
    block = lax.broadcasted_iota(I32, (PAGES, 128), 0)
    sums = jnp.zeros((PAGES, 128), I32)
    for j in range(PAGES):
        got = jnp.max(jnp.where(idx == j, place, 0), axis=0, keepdims=True)
        sums = jnp.where(block == j, got, sums)
    source = jnp.max(sums, axis=1, keepdims=True)
    local = (row == me // 4) & (quarter == me % 4)
    owners = jnp.sum(jnp.where(local, own + 1, 0), axis=0, keepdims=True) - 1
    wide = lax.broadcasted_iota(I32, (PAGES, 128), 1)
    match = owners == block
    low = jnp.min(jnp.where(match, wide % 32, 31), axis=1, keepdims=True)
    high = jnp.max(jnp.where(match, wide % 32, 0), axis=1, keepdims=True)
    tab_v[...] = jnp.where(wide == 0, low, jnp.where(wide == 1, high, source))


def mixer_local(tlen, rate_s, gain_s, x_v, b_v, c_v, step_v, cum_v, full_v, colw_v, y_v, s_v):
    head = lax.broadcasted_iota(I32, (HEADS, BLK), 0)
    rates = jnp.zeros((HEADS, BLK), F32)
    for h in range(HEADS):
        rates = jnp.where(head == h, rate_s[h], rates)
    up = (
        lax.broadcasted_iota(I32, (BLK, BLK), 0) <= lax.broadcasted_iota(I32, (BLK, BLK), 1)
    )
    ones = jnp.where(up, 1.0, 0.0).astype(F32)
    base = jnp.zeros((HEADS, 1), F32)
    when = lax.broadcasted_iota(I32, (HEADS, BLK), 1)
    for b in range(TURN // BLK):
        cols = slice(b * BLK, (b + 1) * BLK)
        step = jnp.where(when + b * BLK < tlen, step_v[:, cols], 0.0)
        step_v[:, cols] = step
        cum = lax.dot_general(
            -rates * step, ones, (((1,), (0,)), ((), ())),
            preferred_element_type=F32, precision=lax.Precision.HIGHEST,
        )
        cum_v[:, cols] = cum
        full_v[:, cols] = cum + base
        base = base + cum[:, BLK - 1 :]
        padded = jnp.concatenate([cum, jnp.zeros((BLK - HEADS, BLK), F32)], axis=0)
        colw_v[cols, :] = padded.T
    s_v[...] = jnp.zeros_like(s_v)

    def block(b, carry):
        at = pl.ds(pl.multiple_of(b * BLK, BLK), BLK)
        for g in range(GRP):
            bb = b_v[g, :, at]
            cb = c_v[g, :, at]
            pairs = jnp.where(up, tn(bb, cb), 0.0)
            state = s_v[g * PER : (g + 1) * PER].reshape(PER * CH, STATE)
            read = jnp.dot(state.astype(BF), cb, preferred_element_type=F32)
            cums = cum_v[g * PER : (g + 1) * PER, at]
            steps = step_v[g * PER : (g + 1) * PER, at]
            cols = colw_v[at, :]
            late = jnp.exp(cums[:, BLK - 1 :] - cums) * steps
            grow = jnp.exp(cums)
            written = []
            for i in range(PER):
                h = g * PER + i
                xh = x_v[h, :, at].astype(F32)
                gaps = jnp.minimum(cums[i : i + 1] - cols[:, h : h + 1], 0.0)
                mix = (pairs * jnp.exp(gaps)).astype(BF)
                xs = (xh * steps[i : i + 1]).astype(BF)
                y = jnp.dot(xs, mix, preferred_element_type=F32)
                y = y + grow[i : i + 1] * read[i * CH : (i + 1) * CH] + gain_s[h] * xh
                y_v[h, :, at] = y
                written.append((xh * late[i : i + 1]).astype(BF))
            added = nt(jnp.concatenate(written, axis=0), bb)
            for i in range(PER):
                h = g * PER + i
                s_v[h] = grow[i : i + 1, BLK - 1 :] * s_v[h] + added[i * CH : (i + 1) * CH]
        return carry

    lax.fori_loop(0, TURN // BLK, block, 0)


def mixer_saved(tlen, tab_s, saved_v, c_v, full_v, y_v, s_v, mix_o, next_o, s0_v):
    def pick(j, carry):
        s0_v[j] = saved_v[tab_s[j, 2]]
        return carry

    lax.fori_loop(0, HEADS, pick, 0)
    when = lax.broadcasted_iota(I32, (CH, TURN), 1)
    for g in range(GRP):
        start = s0_v[g * PER : (g + 1) * PER].reshape(PER * CH, STATE)
        read = jnp.dot(start, c_v[g], preferred_element_type=F32)
        for i in range(PER):
            h = g * PER + i
            grow = jnp.exp(full_v[h : h + 1, :])
            y = y_v[h] + grow * read[i * CH : (i + 1) * CH]
            mix_o[h] = jnp.where(when < tlen, y, 0.0).astype(BF)
            last = grow[:, TURN - 1 :]
            next_o[h] = last * s0_v[h].astype(F32) + s_v[h]


def attend(g, hlen, seg, q_all, k_v, v_v, o_send, l_send, send_part):
    key = lax.broadcasted_iota(I32, (1, HROWS), 1) + seg * HROWS
    seen = jnp.where(key < hlen, 0.0, NEG)
    half = QH // 2
    lane = lax.broadcasted_iota(I32, (TOK, 128), 1)

    def dest(k, carry):
        off = lax.rem(k + 1, CTX)
        c = lax.rem(seg + off, CTX)
        token = lax.broadcasted_iota(I32, (TOK, TOK), 0) + c * TOK
        fresh = lax.broadcasted_iota(I32, (TOK, TOK), 1) + seg * TOK
        turn = jnp.where(fresh <= token, 0.0, NEG)
        turn = jnp.concatenate([turn] * half, axis=0)
        keep = jnp.zeros((TOK, 128), F32)
        for part in range(2):
            first = g * QH + part * half
            q = jnp.concatenate(
                [q_all[c, :, (first + j) * HD : (first + j + 1) * HD] for j in range(half)], axis=0
            )
            s = nt(q, k_v[...]) * SCALE
            sh = s[:, :HROWS] + seen
            st = s[:, HROWS:] + turn
            top = jnp.maximum(
                jnp.max(sh, axis=1, keepdims=True), jnp.max(st, axis=1, keepdims=True)
            )
            ph = jnp.exp2(sh - top).astype(BF)
            pt = jnp.exp2(st - top).astype(BF)
            o = jnp.dot(ph, v_v[:HROWS], preferred_element_type=F32) + jnp.dot(
                pt, v_v[HROWS:], preferred_element_type=F32
            )
            total = o[:, HD:]
            out = (o[:, :HD] / total).astype(BF)
            logs = top + jnp.log2(total)
            for j in range(half):
                at = slice(j * TOK, (j + 1) * TOK)
                n = part * half + j
                o_send[g, k, :, n * HD : (n + 1) * HD] = out[at]
                keep = jnp.where(lane == n, logs[at], keep)
        l_send[g, k] = keep.T[:QH]

        @pl.when(k < CTX - 1)
        def _():
            send_part(g, k, off, c)

        return carry

    lax.fori_loop(0, CTX, dest, 0)


def merge(g, tlen, seg, o_send, l_send, o_recv, l_recv, att_o):
    logs = [l_recv[g, 0], l_recv[g, 1], l_recv[g, 2], l_send[g, CTX - 1]]
    top = functools.reduce(jnp.maximum, logs)
    parts = [jnp.exp2(l - top) for l in logs]
    whole = parts[0] + parts[1] + parts[2] + parts[3]
    shares = jnp.concatenate(
        [p / whole for p in parts] + [jnp.zeros((TOK - CTX * QH, 128), F32)], axis=0
    ).T
    live = lax.broadcasted_iota(I32, (TOK, HD), 0) + seg * TOK < tlen
    for j in range(QH):
        cols = slice(j * HD, (j + 1) * HD)
        out = jnp.zeros((TOK, HD), F32)
        for i in range(CTX):
            part = o_recv[g, i, :, cols] if i < CTX - 1 else o_send[g, CTX - 1, :, cols]
            n = i * QH + j
            out = out + shares[:, n : n + 1] * part.astype(F32)
        base = g * QH * HD
        att_o[:, base + j * HD : base + (j + 1) * HD] = jnp.where(live, out, 0.0).astype(BF)


def kernel(
    rate_s, gain_s, own_r, idx_r, hlen_h, tlen_h,
    kv_h, st_h, x_h, b_h, c_h, step_h, q_h, turn_h,
    mix_o, next_o, att_o,
    hlen_s, tlen_s, kv_v, st_v, x_v, b_v, c_v, step_v, turn_v, tab_v, tab_s,
    kv_send, kv_recv0, kv_recv1, st_send, st_recv, q_all,
    cum_v, full_v, colw_v, y_v, s_v, s0_v, k_v, v_v,
    o_send, l_send, o_recv, l_recv,
    in_sem, tab_sem, kv_ss, kv_rs, st_ss, st_rs, q_ss, q_rs, o_ss, o_rs, l_ss, l_rs,
):
    me = lax.axis_index("pool")
    seg = lax.axis_index("ctx")
    side = lax.axis_index("head")
    row, col = me // 8, me % 8
    kv_recv = (kv_recv0, kv_recv1)

    def peer(i):
        k = lax.rem(i * jnp.where(side % 2 == 0, 5, 27), POOL)
        return lax.rem(row + k // 8, 4) * 8 + lax.rem(col + lax.rem(k, 8), 8)

    barrier = pltpu.get_barrier_semaphore()

    def greet(i, carry):
        pl.semaphore_signal(
            barrier, inc=1, device_id=(peer(i), seg, side), device_id_type=MESH
        )
        return carry

    lax.fori_loop(1, POOL, greet, 0)
    for off in range(1, CTX):
        pl.semaphore_signal(
            barrier, inc=1, device_id=(me, lax.rem(seg + off, CTX), side), device_id_type=MESH
        )

    loads = [
        pltpu.make_async_copy(src, dst, in_sem.at[i])
        for i, (src, dst) in enumerate(
            [
                (kv_h, kv_v), (st_h, st_v), (q_h, q_all.at[seg]), (x_h, x_v), (b_h, b_v),
                (c_h, c_v), (step_h, step_v), (turn_h, turn_v), (hlen_h, hlen_s), (tlen_h, tlen_s),
            ]
        )
    ]
    for load in loads:
        load.start()
    build_tables(own_r[...], idx_r[...], me, tab_v)
    table = pltpu.make_async_copy(tab_v, tab_s, tab_sem)
    table.start()

    def kv_copy(g, i):
        return pltpu.make_async_remote_copy(
            src_ref=kv_send.at[g, pl.ds(2 * i, 2)], dst_ref=kv_recv[g].at[pl.ds(2 * me, 2)],
            send_sem=kv_ss.at[g, i], recv_sem=kv_rs.at[g, i],
            device_id=(peer(i), seg, side), device_id_type=MESH,
        )

    def st_copy(i):
        return pltpu.make_async_remote_copy(
            src_ref=st_send.at[pl.ds(2 * i, 2)], dst_ref=st_recv.at[pl.ds(2 * me, 2)],
            send_sem=st_ss.at[i], recv_sem=st_rs.at[i],
            device_id=(peer(i), seg, side), device_id_type=MESH,
        )

    def q_copy(g, off):
        cols = pl.ds(g * QH * HD, QH * HD)
        return pltpu.make_async_remote_copy(
            src_ref=q_h.at[:, cols], dst_ref=q_all.at[seg, :, cols],
            send_sem=q_ss.at[g, off - 1], recv_sem=q_rs.at[g, off - 1],
            device_id=(me, lax.rem(seg + off, CTX), side), device_id_type=MESH,
        )

    def o_copy(g, k, c):
        return pltpu.make_async_remote_copy(
            src_ref=o_send.at[g, k], dst_ref=o_recv.at[g, k],
            send_sem=o_ss.at[g, k], recv_sem=o_rs.at[g, k],
            device_id=(me, c, side), device_id_type=MESH,
        )

    def l_copy(g, k, c):
        return pltpu.make_async_remote_copy(
            src_ref=l_send.at[g, k], dst_ref=l_recv.at[g, k],
            send_sem=l_ss.at[g, k], recv_sem=l_rs.at[g, k],
            device_id=(me, c, side), device_id_type=MESH,
        )

    def send_part(g, k, off, c):
        o_copy(g, k, c).start()
        l_copy(g, k, c).start()

    def pack_kv(g):
        lanes = slice(g * HD, (g + 1) * HD)

        def pack(i, carry):
            to = peer(i)
            for r in range(2):
                kv_send[g, 2 * i + r] = kv_v[tab_s[to, r], :, :, lanes]
            return carry

        lax.fori_loop(1, POOL, pack, 0)
        for r in range(2):
            kv_recv[g][2 * me + r] = kv_v[tab_s[me, r], :, :, lanes]

    def each(body, first=1, last=POOL):
        def step(i, carry):
            body(i)
            return carry

        lax.fori_loop(first, last, step, 0)

    def arrive_kv(g):
        lanes = slice(g * HD, (g + 1) * HD)
        if g == 0:
            each(lambda i: kv_copy(g, i).wait_recv())

        def place(j):
            page = kv_recv[g][tab_s[j, 2]]
            at = pl.ds(pl.multiple_of(j * PAGE, PAGE), PAGE)
            k_v[at, :] = page[0]
            v_v[at, :HD] = page[1]

        each(place, 0, PAGES)
        k_v[HROWS:, :] = turn_v[0, :, lanes]
        v_v[HROWS:, :HD] = turn_v[1, :, lanes]
        for off in range(1, CTX):
            q_copy(g, off).wait_recv()

    def join(g):
        for k in range(CTX - 1):
            c = lax.rem(seg + k + 1, CTX)
            o_copy(g, k, c).wait_recv()
            l_copy(g, k, c).wait_recv()
        merge(g, tlen_s[0], seg, o_send, l_send, o_recv, l_recv, att_o)

    table.wait()
    loads[0].wait()
    pack_kv(0)
    pl.semaphore_wait(barrier, POOL - 1 + CTX - 1)
    each(lambda i: kv_copy(0, i).start())
    for off in range(1, CTX):
        q_copy(0, off).start()
    for off in range(1, CTX):
        q_copy(1, off).start()
    pack_kv(1)
    loads[1].wait()
    for r in range(2):
        st_recv[2 * me + r] = st_v[tab_s[me, r]]

    def pack_state(i):
        to = peer(i)
        for r in range(2):
            st_send[2 * i + r] = st_v[tab_s[to, r]]

    each(lambda i: kv_copy(1, i).start())
    each(pack_state)
    for load in loads[2:]:
        load.wait()
    hlen, tlen = hlen_s[0], tlen_s[0]
    mixer_local(tlen, rate_s, gain_s, x_v, b_v, c_v, step_v, cum_v, full_v, colw_v, y_v, s_v)
    v_v[:, HD:] = jnp.ones((ROWS, HD), BF)

    def second(i):
        kv_copy(0, i).wait_send()
        kv_copy(1, i).start()

    arrive_kv(0)
    attend(0, hlen, seg, q_all, k_v, v_v, o_send, l_send, send_part)

    def third(i):
        kv_copy(1, i).wait_send()
        st_copy(i).start()

    each(lambda i: kv_copy(1, i).wait_recv())
    each(third)
    arrive_kv(1)
    attend(1, hlen, seg, q_all, k_v, v_v, o_send, l_send, send_part)
    join(0)
    each(lambda i: st_copy(i).wait_recv())
    mixer_saved(tlen, tab_s, st_recv, c_v, full_v, y_v, s_v, mix_o, next_o, s0_v)
    join(1)

    each(lambda i: st_copy(i).wait_send())
    each(lambda i: kv_copy(0, i).wait_send())
    for g in range(KVH):
        for k in range(CTX - 1):
            c = lax.rem(seg + k + 1, CTX)
            q_copy(g, k + 1).wait_send()
            o_copy(g, k, c).wait_send()
            l_copy(g, k, c).wait_send()


def hand_over(a, b, c, x, y, z, u, v, w, sem):
    trips = [(a, u, x), (b, v, y), (c, w, z)]
    there = [pltpu.make_async_copy(src, mid, sem.at[0, i]) for i, (src, mid, _) in enumerate(trips)]
    back = [pltpu.make_async_copy(mid, dst, sem.at[1, i]) for i, (_, mid, dst) in enumerate(trips)]
    for copy in there:
        copy.start()
    for first, then in zip(there, back):
        first.wait()
        then.start()
    for copy in back:
        copy.wait()


def local(
    kv_pool, state_pool, block_owner, block_index, history_len, turn_len, mixer_in, input_proj,
    output_proj, step_size, decay_rate, bypass_factor, queries, turn_kv,
):
    hbm = pl.BlockSpec(memory_space=pl.ANY)
    vmem = pl.BlockSpec(memory_space=pltpu.VMEM)
    smem = pl.BlockSpec(memory_space=pltpu.SMEM)
    dma = pltpu.SemaphoreType.DMA
    outs = (
        jax.ShapeDtypeStruct((HEADS, CH, TURN), BF),
        jax.ShapeDtypeStruct((HEADS, CH, STATE), F32),
        jax.ShapeDtypeStruct((TOK, KVH * QH * HD), BF),
    )
    results = pl.pallas_call(
        kernel,
        out_shape=outs,
        in_specs=[smem] * 2 + [vmem] * 2 + [pl.BlockSpec(memory_space=pltpu.HBM)] * 2 + [hbm] * 8,
        out_specs=(vmem, vmem, vmem),
        scratch_shapes=[
            pltpu.SMEM((1,), I32),
            pltpu.SMEM((1,), I32),
            pltpu.VMEM((PAGES, 2, PAGE, KVH * HD), BF),
            pltpu.VMEM((PAGES, CH, STATE), BF),
            pltpu.VMEM((HEADS, CH, TURN), BF),
            pltpu.VMEM((GRP, STATE, TURN), BF),
            pltpu.VMEM((GRP, STATE, TURN), BF),
            pltpu.VMEM((HEADS, TURN), F32),
            pltpu.VMEM((2, TOK, KVH * HD), BF),
            pltpu.VMEM((PAGES, 128), I32),
            pltpu.SMEM((PAGES, 128), I32),
            pltpu.VMEM((KVH, 2 * POOL, 2, PAGE, HD), BF),
            pltpu.VMEM((2 * POOL, 2, PAGE, HD), BF),
            pltpu.VMEM((2 * POOL, 2, PAGE, HD), BF),
            pltpu.VMEM((2 * POOL, CH, STATE), BF),
            pltpu.VMEM((2 * POOL, CH, STATE), BF),
            pltpu.VMEM((CTX, TOK, KVH * QH * HD), BF),
            pltpu.VMEM((HEADS, TURN), F32),
            pltpu.VMEM((HEADS, TURN), F32),
            pltpu.VMEM((TURN, 128), F32),
            pltpu.VMEM((HEADS, CH, TURN), F32),
            pltpu.VMEM((HEADS, CH, STATE), F32),
            pltpu.VMEM((HEADS, CH, STATE), BF),
            pltpu.VMEM((ROWS, HD), BF),
            pltpu.VMEM((ROWS, 2 * HD), BF),
            pltpu.VMEM((KVH, CTX, TOK, QH * HD), BF),
            pltpu.VMEM((KVH, CTX, QH, TOK), F32),
            pltpu.VMEM((KVH, CTX - 1, TOK, QH * HD), BF),
            pltpu.VMEM((KVH, CTX - 1, QH, TOK), F32),
            dma((10,)), dma(()),
            dma((KVH, POOL)), dma((KVH, POOL)), dma((POOL,)), dma((POOL,)),
            dma((KVH, CTX - 1)), dma((KVH, CTX - 1)), dma((KVH, CTX - 1)), dma((KVH, CTX - 1)),
            dma((KVH, CTX - 1)), dma((KVH, CTX - 1)),
        ],
        compiler_params=pltpu.CompilerParams(
            collective_id=0, has_side_effects=True, vmem_limit_bytes=56 << 20
        ),
        name="resume",
    )(
        decay_rate, bypass_factor,
        block_owner.reshape(8, 128), block_index.reshape(8, 128), history_len, turn_len,
        kv_pool[0], state_pool, mixer_in[0], input_proj[0], output_proj[0], step_size[0],
        queries[0], turn_kv[0],
    )
    mixed, final, attended = pl.pallas_call(
        hand_over,
        out_shape=outs,
        in_specs=[hbm] * 3,
        out_specs=(hbm,) * 3,
        scratch_shapes=[pltpu.VMEM(o.shape, o.dtype) for o in outs] + [dma((2, 3))],
        name="hand_over",
    )(*results)
    return mixed[None], final[None], attended[None]


def solution(mesh):
    return jax.shard_map(
        local,
        mesh=mesh,
        in_specs=(
            P("ctx", "pool", None, None, "head"),
            P("pool", "ctx", "head"),
            P("ctx", None),
            P("ctx", None),
            P("pool"),
            P("pool"),
            P("pool", "head", "ctx", None),
            P("pool", "head", None, None),
            P("pool", "head", None, None),
            P("pool", "head", None),
            P("head"),
            P("head"),
            P("pool", "ctx", "head"),
            P("pool", None, "ctx", "head"),
        ),
        out_specs=(
            P("pool", "head", "ctx", None),
            P("pool", "head", "ctx", None),
            P("pool", "ctx", "head"),
        ),
        check_vma=False,
    )
```
